32 devices in a mesh: seq: 4 (over z), expert: 8 (over y, x, core).
Axes of the slice: x: 2, y: 2, z: 4, core: 2. Of those that a mesh axis runs over, the one named last changes fastest.
Arguments:
- residual: bfloat16 [8, 512, 2048], P('expert', 'seq'), may hold values from -6 to 6
- queries: bfloat16 [8, 512, 2048], P('expert', 'seq'), may hold values from -400 to 400
- key_input: bfloat16 [8, 512, 512], P('expert', 'seq'), may hold values from -4 to 4
- value_input: bfloat16 [8, 512, 512], P('expert', 'seq'), may hold values from -6 to 6
- routes: int32 [8, 512, 6], P('expert', 'seq'), may hold values from 0 to 15, all different within a row; in each aligned block of 128 rows (0 to 127, 128 to 255, ..., all dimensions but the last counted through in order) at most 60 rows name the same one
- mix_weights: float32 [8, 512, 6], P('expert', 'seq'), may hold values from 0.1 to 1
- gate_weight: bfloat16 [16, 2048, 704], P('expert'), may hold values from -0.125 to 0.125
- up_weight: bfloat16 [16, 2048, 704], P('expert'), may hold values from -0.125 to 0.125
- down_weight: bfloat16 [16, 704, 2048], P('expert'), may hold values from -0.21875 to 0.21875
- grad_out: bfloat16 [8, 512, 2048], P('expert', 'seq'), may hold values from -6 to 6
Outputs:
- layer_out: bfloat16 [8, 512, 2048], P('expert', 'seq')
- residual_grad: bfloat16 [8, 512, 2048], P('expert', 'seq')
- query_grad: bfloat16 [8, 512, 2048], P('expert', 'seq')
- key_grad: bfloat16 [8, 512, 512], P('expert', 'seq')
- value_grad: bfloat16 [8, 512, 512], P('expert', 'seq')
- mix_grad: float32 [8, 512, 6], P('expert', 'seq')
- gate_weight_grad: bfloat16 [16, 2048, 704], P('expert', 'seq')
- up_weight_grad: bfloat16 [16, 2048, 704], P('expert', 'seq')
- down_weight_grad: bfloat16 [16, 704, 2048], P('expert', None, 'seq')
The draws below stay inside these ranges and needn't reach their ends.
Inputs may be any that keep to these rules, and one draw needn't show every extreme that they name: `routes`: each row names 6 different experts. Among the rows of one device no expert is named by more than 60 rows, and in every draw some expert is named by exactly 60 rows of some device.
All inputs are finite; a program needn't handle non-finite values.
Results may differ from the reference program's by a relative error of at most 0.04.
Values may be sent and summed in bfloat16 or wider, within the bound.
A program may use at most 192 MiB of HBM per device.

```python
import math
import jax
import jax.numpy as jnp
import numpy as np
from jax import lax

D = 2048
HQ = 16
HK = 4
DH = 128
F = 704
TOPK = 6
TOK_DEV = 128
EXPERTS = 16
SEQS = 8
SEQ_LEN = 512
CAP = 60
N_SEQ = 4


def paired_draws(key):
    key_base = jax.random.fold_in(key, 101)
    query_base = jax.random.fold_in(key, 202)
    key_vectors = jnp.clip(jax.random.normal(key_base, (SEQS, SEQ_LEN, HK, DH), jnp.float32), -4.0, 4.0)
    query_vectors = jnp.clip(jax.random.normal(query_base, (SEQS, SEQ_LEN, HQ, DH), jnp.float32), -4.0, 4.0)
    query_out = query_vectors.reshape(SEQS, SEQ_LEN, HQ * DH).astype(jnp.bfloat16)
    key_out = key_vectors.reshape(SEQS, SEQ_LEN, HK * DH).astype(jnp.bfloat16)
    return (query_out, key_out)


def draw_queries(key, part):
    return paired_draws(key)[0]


def draw_key_input(key, part):
    return paired_draws(key)[1]


def shard_levels(stream_key, shape, pieces, low, largest):
    gain = 1.0
    for axis_at, blocks in pieces:
        steps = jax.random.uniform(jax.random.fold_in(jax.random.fold_in(stream_key, 6), axis_at), (blocks,), jnp.float32, low / len(pieces), largest / len(pieces))
        gain = gain * jnp.repeat(jnp.exp(steps), shape[axis_at] // blocks).reshape((-1,) + (1,) * (len(shape) - 1 - axis_at))
    return gain


def routed_block(own_key, own, number, rows, count, top, bound, lean):
    ranking = jax.random.permutation(own_key, count)
    heavy_load, ordinary = portions_of(count, rows * top, bound, lean, True), portions_of(count, rows * top, bound, lean, False)
    places = jnp.arange(count)

    def named(sizes, turn):
        used = int((sizes > 0).sum())
        fixed = max(1, used // 4)
        moved = fixed + (places - fixed + turn * (used - fixed)) % max(1, count - fixed)
        return jnp.zeros((count,), jnp.int32).at[ranking[jnp.where(places < fixed, places, moved)]].set(jnp.asarray(sizes, jnp.int32))

    sizes = jnp.where(number % 4 == 0, named(heavy_load, number // 4), named(ordinary, number - number // 4 - 1))
    mixed = jax.random.permutation(jax.random.fold_in(own, 3), count)
    giver, sink = mixed[0:count // 2 * 2:2], mixed[1:count // 2 * 2:2]
    margin = jnp.minimum(sizes[giver] - 1, bound - sizes[sink]) // 2
    margin = jnp.where((giver == ranking[0]) | (sink == ranking[0]) | (sizes[sink] == 0), 0, jnp.maximum(margin, 0))
    moved = jax.random.randint(jax.random.fold_in(own, 4), (count // 2,), 0, 1 << 20) % (margin + 1)
    sizes = sizes.at[giver].add(-moved).at[sink].add(moved)
    members = jnp.searchsorted(jnp.cumsum(sizes), jnp.arange(rows * top), side="right").astype(jnp.int32)
    grid = members.reshape(top, rows).T
    grid = grid[jax.random.permutation(jax.random.fold_in(own, 1), rows)]
    turn = jax.random.randint(jax.random.fold_in(own, 2), (rows, 1), 0, top)
    return jnp.take_along_axis(grid, (jnp.arange(top)[None, :] + turn) % top, axis=1)


def portions_of(amount, total, most, slope, full):
    portions = [(1 << 20) // math.isqrt(standing ** slope) + 1 for standing in range(1, amount + 1)]
    largest = most if full else min(most, max(-(-total // amount), total * portions[0] // sum(portions)))
    least = 1 if total - largest >= amount - 1 else 0
    given, surplus = [largest] + [least] * (amount - 1), total - largest - least * (amount - 1)
    while surplus > 0:
        candidates = [i for i in range(1, amount) if given[i] < largest] or [i for i in range(1, amount) if given[i] < most]
        whole, left = sum([portions[i] for i in candidates]), surplus
        for i in candidates:
            more = min(most - given[i], max(1, left * portions[i] // whole), surplus)
            given[i] = given[i] + more
            surplus = surplus - more
    return np.array(given)


def centred(stream_key, dims, deviation, bound, split=(), held_as=jnp.bfloat16):
    values = deviation * jax.random.normal(stream_key, dims, jnp.float32)
    if split:
        values = values * shard_levels(stream_key, dims, split, -0.22, 0.18)
    return jnp.clip(values, -bound, bound).astype(held_as)


def setup_inputs(seed: int = 0) -> dict:
    splits = jax.random.split(jax.random.key(seed), 11)
    residual = centred(splits[0], (SEQS, SEQ_LEN, D), 1.0, 6.0, ((0, 8), (1, 4)))
    queries = draw_queries(jax.random.fold_in(splits[10], 71), 0)
    key_input = draw_key_input(jax.random.fold_in(splits[10], 71), 0)
    value_input = centred(splits[3], (SEQS, SEQ_LEN, HK * DH), 1.0, 6.0, ((0, 8), (1, 4)))
    routes_keys = jax.random.split(jax.random.fold_in(splits[4], 1), SEQS * SEQ_LEN // TOK_DEV)
    routes_turns = jax.random.permutation(jax.random.fold_in(splits[4], 3), SEQS * SEQ_LEN // TOK_DEV)
    routes = jax.vmap(lambda own, number: routed_block(jax.random.fold_in(splits[4], 2), own, number, TOK_DEV, EXPERTS, TOPK, CAP, 2))(routes_keys, routes_turns).reshape((SEQS, SEQ_LEN, TOPK))
    mix_weights = jnp.clip(jnp.exp(math.log(1.0) - 2.3025851 * jax.random.uniform(splits[5], (SEQS, SEQ_LEN, TOPK), jnp.float32) ** shard_levels(splits[5], (SEQS, SEQ_LEN, TOPK), ((0, 8), (1, 4)), -0.2, 0.2)), 0.1, 1.0)
    gate_weight = centred(splits[6], (EXPERTS, D, F), D ** -0.5, 0.125, ((0, 8),))
    up_weight = centred(splits[7], (EXPERTS, D, F), D ** -0.5, 0.125, ((0, 8),))
    down_weight = centred(splits[8], (EXPERTS, F, D), F ** -0.5, 0.21875, ((0, 8),))
    grad_out = centred(splits[9], (SEQS, SEQ_LEN, D), 1.0, 6.0, ((0, 8), (1, 4)))
    return dict(residual=residual, queries=queries, key_input=key_input, value_input=value_input, routes=routes, mix_weights=mix_weights, gate_weight=gate_weight, up_weight=up_weight, down_weight=down_weight, grad_out=grad_out)


neg_big = -1e+30
norm_eps = 1e-06
highest = lax.Precision.HIGHEST

def round_trip(values):
    return lax.optimization_barrier(values.astype(jnp.bfloat16)).astype(jnp.float32)

def causal_scores(query_seq, key_seq):
    length = query_seq.shape[0]
    group_size = HQ // HK
    query_heads = query_seq.astype(jnp.float32).reshape(length, HK, group_size, DH)
    key_heads = key_seq.astype(jnp.float32).reshape(length, HK, DH)
    scores = jnp.einsum('tkgd,jkd->tkgj', query_heads, key_heads, precision=highest) * (1.0 / math.sqrt(DH))
    positions = jnp.arange(length, dtype=jnp.int32)
    visible = (positions[None, :] <= positions[:, None])[:, None, None, :]
    return (query_heads, key_heads, scores, visible)

def attend_forward(operands):
    query_seq, key_seq, value_seq = operands
    length = query_seq.shape[0]
    query_heads, key_heads, scores, visible = causal_scores(query_seq, key_seq)
    value_heads = value_seq.astype(jnp.float32).reshape(length, HK, DH)
    masked = jnp.where(visible, scores, neg_big)
    row_max = lax.optimization_barrier(jnp.max(masked, axis=3))
    weights = jnp.where(visible, jnp.exp(masked - row_max[..., None]), 0.0)
    row_sum = lax.optimization_barrier(jnp.sum(weights, axis=3))
    mixed = jnp.einsum('tkgj,jkd->tkgd', round_trip(weights), value_heads, precision=highest)
    attention = (mixed / row_sum[..., None]).reshape(length, HQ * DH).astype(jnp.bfloat16)
    return (attention, row_max + jnp.log(row_sum))

def attend_backward(operands):
    query_seq, key_seq, value_seq, attention_seq, total_seq, out_grad_seq = operands
    length = query_seq.shape[0]
    group_size = HQ // HK
    inv_scale = 1.0 / math.sqrt(DH)
    query_heads, key_heads, scores, visible = causal_scores(query_seq, key_seq)
    value_heads = value_seq.astype(jnp.float32).reshape(length, HK, DH)
    probabilities = jnp.where(visible, jnp.exp(scores - total_seq[..., None]), 0.0)
    out_grad = out_grad_seq.astype(jnp.float32).reshape(length, HK, group_size, DH)
    attention_heads = attention_seq.astype(jnp.float32).reshape(length, HK, group_size, DH)
    row_delta = lax.optimization_barrier(jnp.sum(out_grad * attention_heads, axis=3))
    prob_grad = jnp.einsum('tkgd,jkd->tkgj', out_grad, value_heads, precision=highest)
    score_grad = round_trip(probabilities * (prob_grad - row_delta[..., None]))
    query_grad = jnp.einsum('tkgj,jkd->tkgd', score_grad, key_heads, precision=highest) * inv_scale
    blocks_shape = (N_SEQ, TOK_DEV, HK, group_size)
    key_part = jnp.einsum('stkgj,stkgd->sjkd', score_grad.reshape(blocks_shape + (length,)), query_heads.reshape(blocks_shape + (DH,)), precision=highest) * inv_scale
    value_part = jnp.einsum('stkgj,stkgd->sjkd', round_trip(probabilities).reshape(blocks_shape + (length,)), out_grad.reshape(blocks_shape + (DH,)), precision=highest)
    key_grad = lax.optimization_barrier(jnp.sum(round_trip(key_part), axis=0)).reshape(length, HK * DH).astype(jnp.bfloat16)
    value_grad = lax.optimization_barrier(jnp.sum(round_trip(value_part), axis=0)).reshape(length, HK * DH).astype(jnp.bfloat16)
    return (query_grad.reshape(length, HQ * DH).astype(jnp.bfloat16), key_grad, value_grad)

def reference(residual, queries, key_input, value_input, routes, mix_weights, gate_weight, up_weight, down_weight, grad_out):
    attention, log_total = lax.map(attend_forward, (queries, key_input, value_input))
    tokens_all = SEQS * SEQ_LEN
    hidden_flat = (residual.astype(jnp.float32) + attention.astype(jnp.float32)).reshape(tokens_all, D)
    inv_rms = lax.rsqrt(lax.optimization_barrier(jnp.mean(hidden_flat * hidden_flat, axis=1, keepdims=True)) + norm_eps)
    normed = hidden_flat * inv_rms
    normed_bf = normed.astype(jnp.bfloat16)
    blocks = tokens_all // TOK_DEV
    route_blocks = routes.reshape(blocks, TOK_DEV, TOPK)
    onehot = (route_blocks[..., None] == jnp.arange(EXPERTS, dtype=jnp.int32)).astype(jnp.int32)
    per_token = lax.optimization_barrier(jnp.sum(onehot, axis=2))
    earlier = jnp.cumsum(per_token, axis=1) - per_token
    slot_rank = lax.optimization_barrier(jnp.sum(onehot * earlier[:, :, None, :], axis=3))
    position = jnp.arange(blocks, dtype=jnp.int32)[:, None, None] * CAP + slot_rank
    pair_ids = jnp.arange(tokens_all * TOPK, dtype=jnp.int32)
    table = jnp.zeros((EXPERTS, blocks * CAP), jnp.int32).at[route_blocks.reshape(-1), position.reshape(-1)].set(pair_ids)
    alive_table = jnp.zeros((EXPERTS, blocks * CAP), jnp.bool_).at[route_blocks.reshape(-1), position.reshape(-1)].set(True)
    mix_flat = mix_weights.reshape(-1)
    grad_flat = grad_out.reshape(tokens_all, D)

    def forward_step(carried, operands):
        combined, mix_grad = carried
        gate_matrix, up_matrix, down_matrix, pairs, alive = operands
        token_ids = pairs // TOPK
        rows = jnp.where(alive[:, None], normed_bf[token_ids], jnp.zeros((), jnp.bfloat16))
        gate_pre = jnp.dot(rows, gate_matrix, preferred_element_type=jnp.float32)
        up_pre = jnp.dot(rows, up_matrix, preferred_element_type=jnp.float32)
        activation = (jax.nn.silu(gate_pre) * up_pre).astype(jnp.bfloat16)
        output = jnp.dot(activation, down_matrix, preferred_element_type=jnp.float32).astype(jnp.bfloat16)
        weight = jnp.where(alive, mix_flat[pairs], 0.0)
        combined = combined.at[token_ids].add(weight[:, None] * output.astype(jnp.float32))
        inner = lax.optimization_barrier(jnp.sum(grad_flat[token_ids].astype(jnp.float32) * output.astype(jnp.float32), axis=1))
        mix_grad = mix_grad.at[pairs].add(jnp.where(alive, inner, 0.0))
        return ((combined, mix_grad), None)
    (combined, mix_grad), ignored = lax.scan(forward_step, (hidden_flat, jnp.zeros((tokens_all * TOPK,), jnp.float32)), (gate_weight, up_weight, down_weight, table, alive_table))

    def backward_step(normed_grad, operands):
        gate_matrix, up_matrix, down_matrix, pairs, alive = operands
        token_ids = pairs // TOPK
        rows = jnp.where(alive[:, None], normed_bf[token_ids], jnp.zeros((), jnp.bfloat16))
        gate_pre = jnp.dot(rows, gate_matrix, preferred_element_type=jnp.float32)
        up_pre = jnp.dot(rows, up_matrix, preferred_element_type=jnp.float32)
        activation = (jax.nn.silu(gate_pre) * up_pre).astype(jnp.bfloat16)
        weight = jnp.where(alive, mix_flat[pairs], 0.0)
        grad_rows = (weight[:, None] * grad_flat[token_ids].astype(jnp.float32)).astype(jnp.bfloat16)
        act_grad = jnp.dot(grad_rows, down_matrix.T, preferred_element_type=jnp.float32)
        sigmoid = jax.nn.sigmoid(gate_pre)
        gate_grad = (act_grad * up_pre * sigmoid * (1.0 + gate_pre * (1.0 - sigmoid))).astype(jnp.bfloat16)
        up_grad = (act_grad * gate_pre * sigmoid).astype(jnp.bfloat16)
        input_grad = (jnp.dot(gate_grad, gate_matrix.T, preferred_element_type=jnp.float32) + jnp.dot(up_grad, up_matrix.T, preferred_element_type=jnp.float32)).astype(jnp.bfloat16)
        normed_grad = normed_grad.at[token_ids].add(jnp.where(alive[:, None], input_grad.astype(jnp.float32), 0.0))
        rows_split = rows.astype(jnp.float32).reshape(SEQS, N_SEQ, CAP, D)
        gate_split = gate_grad.astype(jnp.float32).reshape(SEQS, N_SEQ, CAP, F)
        up_split = up_grad.astype(jnp.float32).reshape(SEQS, N_SEQ, CAP, F)
        act_split = activation.astype(jnp.float32).reshape(SEQS, N_SEQ, CAP, F)
        grad_split = grad_rows.astype(jnp.float32).reshape(SEQS, N_SEQ, CAP, D)
        gate_part = jnp.einsum('jscd,jscf->sdf', rows_split, gate_split, precision=highest)
        up_part = jnp.einsum('jscd,jscf->sdf', rows_split, up_split, precision=highest)
        down_part = jnp.einsum('jscf,jscd->sfd', act_split, grad_split, precision=highest)
        sums = (lax.optimization_barrier(jnp.sum(round_trip(gate_part), axis=0)).astype(jnp.bfloat16), lax.optimization_barrier(jnp.sum(round_trip(up_part), axis=0)).astype(jnp.bfloat16), lax.optimization_barrier(jnp.sum(round_trip(down_part), axis=0)).astype(jnp.bfloat16))
        return (normed_grad, sums)
    normed_grad, weight_sums = lax.scan(backward_step, jnp.zeros((tokens_all, D), jnp.float32), (gate_weight, up_weight, down_weight, table, alive_table))
    dot_mean = lax.optimization_barrier(jnp.mean(normed_grad * normed, axis=1, keepdims=True))
    hidden_grad = grad_flat.astype(jnp.float32) + inv_rms * (normed_grad - normed * dot_mean)
    residual_grad = hidden_grad.astype(jnp.bfloat16).reshape(SEQS, SEQ_LEN, D)
    query_grad, key_grad, value_grad = lax.map(attend_backward, (queries, key_input, value_input, attention, log_total, residual_grad))
    layer_out = combined.astype(jnp.bfloat16).reshape(SEQS, SEQ_LEN, D)
    return (layer_out, residual_grad, query_grad, key_grad, value_grad, mix_grad.reshape(SEQS, SEQ_LEN, TOPK), weight_sums[0], weight_sums[1], weight_sums[2])
```

```python
import functools
import math

import jax
import jax.numpy as jnp
from jax import lax
from jax.experimental import pallas as pl
from jax.experimental.pallas import tpu as pltpu
from jax.sharding import PartitionSpec as P

DH = 128
neg_big = -1e30
norm_eps = 1e-06
BF = jnp.bfloat16
F32 = jnp.float32
GATHER_BYTES = 32 * 1024 * 1024
VMEM_LIMIT = 56 * 1024 * 1024


def dot(a, b, ca, cb):
    return lax.dot_general(a, b, (((ca,), (cb,)), ((), ())), preferred_element_type=F32)


def vm():
    return pl.BlockSpec(memory_space=pltpu.VMEM)


def heads_of(ref, first, count):
    return jnp.concatenate(
        [ref[:, (first + g) * DH : (first + g + 1) * DH] for g in range(count)], axis=0
    )


def visible_mask(tokens, group, full, seq_index):
    shape = (group, tokens, full)
    pos = lax.broadcasted_iota(jnp.int32, shape, 1) + seq_index * tokens
    key = lax.broadcasted_iota(jnp.int32, shape, 2)
    return (key <= pos).reshape(group * tokens, full)


def attend_kernel(group, residual, q, kv, att, log_total, inv_rms, normed):
    tokens = q.shape[0]
    full = kv.shape[0]
    kv_heads = kv.shape[1] // (2 * DH)
    visible = visible_mask(tokens, group, full, lax.axis_index("seq"))
    scale = 1.0 / math.sqrt(DH)
    for k in range(kv_heads):
        qh = heads_of(q, k * group, group)
        kh = kv[:, k * DH : (k + 1) * DH]
        vh = kv[:, (kv_heads + k) * DH : (kv_heads + k + 1) * DH]
        scores = jnp.where(visible, dot(qh, kh, 1, 1) * scale, neg_big)
        top = jnp.max(scores, axis=1, keepdims=True)
        weights = jnp.exp(scores - top)
        total = jnp.sum(weights, axis=1, keepdims=True)
        out = (dot(weights.astype(BF), vh, 1, 0) / total).astype(BF)
        logs = top + jnp.log(total)
        for g in range(group):
            h = k * group + g
            att[:, h * DH : (h + 1) * DH] = out[g * tokens : (g + 1) * tokens]
            log_total[:, h : h + 1] = logs[g * tokens : (g + 1) * tokens]
    hidden = residual[...].astype(F32) + att[...].astype(F32)
    inv = lax.rsqrt(jnp.mean(hidden * hidden, axis=1, keepdims=True) + norm_eps)
    inv_rms[...] = inv
    normed[...] = (hidden * inv).astype(BF)


def attend(residual, q, kv, group):
    tokens, width = q.shape
    heads = width // DH
    return pl.pallas_call(
        functools.partial(attend_kernel, group),
        out_shape=(
            jax.ShapeDtypeStruct((tokens, width), BF),
            jax.ShapeDtypeStruct((tokens, heads), F32),
            jax.ShapeDtypeStruct((tokens, 1), F32),
            jax.ShapeDtypeStruct((tokens, width), BF),
        ),
        in_specs=[vm()] * 3,
        out_specs=(vm(),) * 4,
        compiler_params=pltpu.CompilerParams(vmem_limit_bytes=VMEM_LIMIT),
        cost_estimate=pl.CostEstimate(
            flops=4 * tokens * kv.shape[0] * width,
            bytes_accessed=8 * tokens * width + 2 * kv.size,
            transcendentals=heads * tokens * kv.shape[0],
        ),
        name="attend",
    )(residual, q, kv)


def attend_back_kernel(
    group, residual, q, kv, att, log_total, inv_rms, grad_out, normed_grad, res_grad, q_grad, kv_part
):
    tokens = q.shape[0]
    full = kv.shape[0]
    kv_heads = kv.shape[1] // (2 * DH)
    scale = 1.0 / math.sqrt(DH)
    inv = inv_rms[...]
    normed = (residual[...].astype(F32) + att[...].astype(F32)) * inv
    ngrad = normed_grad[...].astype(F32)
    dot_mean = jnp.mean(ngrad * normed, axis=1, keepdims=True)
    res_grad[...] = (grad_out[...].astype(F32) + inv * (ngrad - normed * dot_mean)).astype(BF)
    visible = visible_mask(tokens, group, full, lax.axis_index("seq"))
    for k in range(kv_heads):
        qh = heads_of(q, k * group, group)
        oh = heads_of(att, k * group, group)
        gh = heads_of(res_grad, k * group, group)
        logs = jnp.concatenate(
            [log_total[:, k * group + g : k * group + g + 1] for g in range(group)], axis=0
        )
        kh = kv[:, k * DH : (k + 1) * DH]
        vh = kv[:, (kv_heads + k) * DH : (kv_heads + k + 1) * DH]
        scores = jnp.where(visible, dot(qh, kh, 1, 1) * scale, neg_big)
        probs = jnp.exp(scores - logs)
        delta = jnp.sum(gh.astype(F32) * oh.astype(F32), axis=1, keepdims=True)
        pgrad = dot(gh, vh, 1, 1)
        sgrad = (probs * (pgrad - delta)).astype(BF)
        dq = (dot(sgrad, kh, 1, 0) * scale).astype(BF)
        for g in range(group):
            h = k * group + g
            q_grad[:, h * DH : (h + 1) * DH] = dq[g * tokens : (g + 1) * tokens]
        kv_part[:, k * DH : (k + 1) * DH] = (dot(sgrad, qh, 0, 0) * scale).astype(BF)
        kv_part[:, (kv_heads + k) * DH : (kv_heads + k + 1) * DH] = dot(
            probs.astype(BF), gh, 0, 0
        ).astype(BF)


def attend_back(group, residual, q, kv, att, log_total, inv_rms, grad_out, normed_grad):
    tokens, width = q.shape
    return pl.pallas_call(
        functools.partial(attend_back_kernel, group),
        out_shape=(
            jax.ShapeDtypeStruct((tokens, width), BF),
            jax.ShapeDtypeStruct((tokens, width), BF),
            jax.ShapeDtypeStruct(kv.shape, BF),
        ),
        in_specs=[vm()] * 8,
        out_specs=(vm(),) * 3,
        compiler_params=pltpu.CompilerParams(vmem_limit_bytes=VMEM_LIMIT),
        cost_estimate=pl.CostEstimate(
            flops=10 * tokens * kv.shape[0] * width,
            bytes_accessed=14 * tokens * width + 4 * kv.size,
            transcendentals=tokens * kv.shape[0] * (width // DH),
        ),
        name="attend_back",
    )(residual, q, kv, att, log_total, inv_rms, grad_out, normed_grad)


def pick_kernel(seq_index, slot, rows, picked):
    local = slot.shape[2]
    depth = picked.shape[1]
    tokens = rows.shape[2]
    row = lax.broadcasted_iota(jnp.int32, (depth, tokens), 0)
    for e in range(local):
        chosen = (slot[0, 0, e : e + 1, :] == row).astype(F32).astype(BF)
        picked[e] = dot(chosen, rows[0, 0], 1, 0).astype(BF)


def pick_rows(gathered, slot, seq_index, first, planes, depth):
    seqs, ranks, tokens, width = gathered.shape
    local = slot.shape[2]
    count = planes * ranks

    def source(i, s):
        return (lax.rem(s[0] + first + i // ranks, seqs), lax.rem(i, ranks), 0, 0)

    return pl.pallas_call(
        pick_kernel,
        out_shape=jax.ShapeDtypeStruct((local, count * depth, width), BF),
        grid_spec=pltpu.PrefetchScalarGridSpec(
            num_scalar_prefetch=1,
            grid=(count,),
            in_specs=[
                pl.BlockSpec((1, 1, local, tokens), source),
                pl.BlockSpec((1, 1, tokens, width), source),
            ],
            out_specs=pl.BlockSpec((local, depth, width), lambda i, s: (0, i, 0)),
        ),
        compiler_params=pltpu.CompilerParams(vmem_limit_bytes=16 * 1024 * 1024),
        cost_estimate=pl.CostEstimate(
            flops=2 * local * count * depth * tokens * width,
            bytes_accessed=2 * count * (tokens + local * depth) * width,
            transcendentals=0,
        ),
        name="pick_rows",
    )(seq_index, slot, gathered)


def spread_kernel(slot, rows, out):
    ranks, local, tokens = slot.shape
    depth = rows.shape[1]
    row = lax.broadcasted_iota(jnp.int32, (depth, tokens), 0)
    total = None
    for e in range(local):
        chosen = (slot[0, e : e + 1, :] == row).astype(F32).astype(BF)
        part = dot(chosen, rows[e], 0, 0)
        total = part if total is None else total + part
    out[0] = total.astype(BF)


def spread_rows(rows, slot):
    ranks, local, tokens = slot.shape
    width = rows.shape[2]
    depth = rows.shape[1] // ranks
    return pl.pallas_call(
        spread_kernel,
        out_shape=jax.ShapeDtypeStruct((ranks, tokens, width), BF),
        grid=(ranks,),
        in_specs=[
            pl.BlockSpec((1, local, tokens), lambda i: (i, 0, 0)),
            pl.BlockSpec((local, depth, width), lambda i: (0, i, 0)),
        ],
        out_specs=pl.BlockSpec((1, tokens, width), lambda i: (i, 0, 0)),
        compiler_params=pltpu.CompilerParams(vmem_limit_bytes=16 * 1024 * 1024),
        cost_estimate=pl.CostEstimate(
            flops=2 * local * ranks * depth * tokens * width,
            bytes_accessed=2 * ranks * (tokens + local * depth) * width,
            transcendentals=0,
        ),
        name="spread_rows",
    )(slot, rows)


def hidden_units(rows, grads, mix, gate_weight, up_weight, down_weight):
    gate_pre = jnp.einsum("erd,edf->erf", rows, gate_weight, preferred_element_type=F32)
    up_pre = jnp.einsum("erd,edf->erf", rows, up_weight, preferred_element_type=F32)
    raw = jnp.einsum("erd,efd->erf", grads, down_weight, preferred_element_type=F32)
    sigmoid = jax.nn.sigmoid(gate_pre)
    silu = gate_pre * sigmoid
    act = silu * up_pre
    act_grad = raw * mix[:, :, None]
    gate_grad = (act_grad * up_pre * sigmoid * (1.0 + gate_pre * (1.0 - sigmoid))).astype(BF)
    up_grad = (act_grad * silu).astype(BF)
    mixed = (act * mix[:, :, None]).astype(BF)
    return (gate_grad, up_grad, mixed, act, raw)


def on_device(
    residual,
    queries,
    key_input,
    value_input,
    routes,
    mix_weights,
    gate_weight,
    up_weight,
    down_weight,
    grad_out,
):
    tokens = residual.shape[1]
    width = residual.shape[2]
    kv_width = key_input.shape[2]
    group = queries.shape[2] // kv_width
    local = gate_weight.shape[0]
    ranks = lax.axis_size("expert")
    seqs = lax.axis_size("seq")
    experts = local * ranks
    top_count = routes.shape[2]
    capacity = tokens * top_count * 5 // (4 * experts)
    depth = -(-capacity // 16) * 16
    both = ("seq", "expert")
    seq_index = lax.axis_index("seq")
    rank_index = lax.axis_index("expert")
    seq_array = seq_index.astype(jnp.int32).reshape(1)

    kv_mine = jnp.concatenate(
        [key_input.reshape(tokens, kv_width), value_input.reshape(tokens, kv_width)], axis=1
    )
    kv = lax.all_gather(kv_mine, "seq", axis=0, tiled=True)

    expert_ids = jnp.arange(experts, dtype=jnp.int32)
    picked = routes.reshape(tokens, top_count)
    mix_rows = mix_weights.reshape(tokens, top_count)
    hit = picked[None, :, :] == expert_ids[:, None, None]
    table = jnp.sum(jnp.where(hit, mix_rows[None], 0.0), axis=2) - (
        1.0 - jnp.sum(hit.astype(F32), axis=2)
    )
    tables = lax.all_gather(table, both, axis=0, tiled=False)
    mine = lax.dynamic_slice_in_dim(tables, rank_index * local, local, axis=1)
    routed = mine >= 0.0
    before = jnp.triu(jnp.ones((tokens, tokens), BF), 1)
    rank = jnp.einsum("bet,tu->beu", routed.astype(BF), before, preferred_element_type=F32)
    slot = jnp.where(routed, rank.astype(jnp.int32), -1)
    slot = slot.reshape(seqs, ranks, local, tokens)
    mine = mine.reshape(seqs, ranks, local, tokens)

    grad_rows = grad_out.reshape(tokens, width)
    grads_all = lax.all_gather(grad_rows, both, axis=0, tiled=True)
    grads_all = grads_all.reshape(seqs, ranks, tokens, width)

    q = queries.reshape(tokens, width)
    res = residual.reshape(tokens, width)
    att, log_total, inv_rms, normed_bf = attend(res, q, kv, group)
    grads_own = pick_rows(grads_all, slot, seq_array, 0, 1, depth)
    grads_far = pick_rows(grads_all, slot, seq_array, 1, seqs - 1, depth)
    if 2 * grads_all.size > GATHER_BYTES:
        normed_bf, grads_own, grads_far = lax.optimization_barrier(
            (normed_bf, grads_own, grads_far)
        )
    normed_all = lax.all_gather(normed_bf, both, axis=0, tiled=True)
    normed_all = normed_all.reshape(seqs, ranks, tokens, width)

    slot_turned = jnp.roll(slot, -seq_index, axis=0)
    mix_turned = jnp.roll(mine, -seq_index, axis=0)
    here = slot_turned[..., None, :] == jnp.arange(depth, dtype=jnp.int32)[:, None]
    mix_slot = jnp.sum(jnp.where(here, mix_turned[..., None, :], 0.0), axis=4)
    mix_slot = jnp.transpose(mix_slot, (2, 0, 1, 3)).reshape(local, seqs * ranks * depth)
    own = ranks * depth

    rows_own = pick_rows(normed_all, slot, seq_array, 0, 1, depth)
    rows_far = pick_rows(normed_all, slot, seq_array, 1, seqs - 1, depth)
    weights = (gate_weight, up_weight, down_weight)
    gate_own, up_own, mixed_own, act_own, raw_own = hidden_units(
        rows_own, grads_own, mix_slot[:, :own], *weights
    )
    input_grad = (
        jnp.einsum("erf,edf->erd", gate_own, gate_weight, preferred_element_type=F32)
        + jnp.einsum("erf,edf->erd", up_own, up_weight, preferred_element_type=F32)
    ).astype(BF)
    slot_own = slot_turned[0]
    input_part = spread_rows(input_grad, slot_own).reshape(ranks * tokens, width)
    normed_grad = lax.psum_scatter(input_part, "expert", scatter_dimension=0, tiled=True)

    expert_out = jnp.einsum(
        "erf,efd->erd", mixed_own, down_weight, preferred_element_type=F32
    ).astype(BF)
    out_part = spread_rows(expert_out, slot_own).reshape(ranks * tokens, width)
    routed_out = lax.psum_scatter(out_part, "expert", scatter_dimension=0, tiled=True)
    hidden = res.astype(F32) + att.astype(F32)
    layer_out = (hidden + routed_out.astype(F32)).astype(BF)

    pair_dot = jnp.sum(act_own.astype(BF).astype(F32) * raw_own, axis=2)
    pair_dot = pair_dot.reshape(local, ranks, depth)
    token_dot = jnp.sum(
        jnp.where(here[0], jnp.transpose(pair_dot, (1, 0, 2))[..., None], 0.0), axis=2
    )
    dots = lax.all_to_all(token_dot, "expert", split_axis=0, concat_axis=0, tiled=True)
    dots = dots.reshape(experts, tokens)
    mix_grad = jnp.sum(jnp.where(hit, dots[:, :, None], 0.0), axis=0)

    gate_far, up_far, mixed_far, _, _ = hidden_units(
        rows_far, grads_far, mix_slot[:, own:], *weights
    )
    share = width // seqs

    def columns(array):
        return lax.dynamic_slice_in_dim(array, seq_index * share, share, axis=2)

    def outer(a_own, a_far, b_own, b_far):
        return (
            jnp.einsum("erm,ern->emn", a_own, b_own, preferred_element_type=F32)
            + jnp.einsum("erm,ern->emn", a_far, b_far, preferred_element_type=F32)
        ).astype(BF)

    cols_own, cols_far = columns(rows_own), columns(rows_far)
    gate_share = outer(cols_own, cols_far, gate_own, gate_far)
    up_share = outer(cols_own, cols_far, up_own, up_far)
    down_share = outer(mixed_own, mixed_far, columns(grads_own), columns(grads_far))

    res_grad, q_grad, kv_part = attend_back(
        group, res, q, kv, att, log_total, inv_rms, grad_rows, normed_grad
    )
    kv_share = lax.psum_scatter(kv_part, "seq", scatter_dimension=0, tiled=True)
    return (
        layer_out.reshape(1, tokens, width),
        res_grad.reshape(1, tokens, width),
        q_grad.reshape(1, tokens, width),
        kv_share[:, :kv_width].reshape(1, tokens, kv_width),
        kv_share[:, kv_width:].reshape(1, tokens, kv_width),
        mix_grad.reshape(1, tokens, top_count),
        gate_share,
        up_share,
        down_share,
    )


def solution(mesh):
    rows = P("expert", "seq", None)
    weight = P("expert", None, None)
    return jax.shard_map(
        on_device,
        mesh=mesh,
        in_specs=(rows,) * 6 + (weight,) * 3 + (rows,),
        out_specs=(rows,) * 8 + (P("expert", None, "seq"),),
        check_vma=False,
    )
```
